32 devices in a mesh: lon: 8 (over y, x, core), lat: 4 (over z).
Axes of the slice: x: 2, y: 2, z: 4, core: 2. Of those that a mesh axis runs over, the one named last changes fastest.
Arguments:
- latent: bfloat16 [4, 64, 128, 320], P(None, 'lat', 'lon'), may hold values from -28 to 28, as said below
- norm1_gain: float32 [320], replicated, may hold values from 0.1 to 1.9
- norm1_shift: float32 [320], replicated, may hold values from -3 to 3
- conv1_weight: bfloat16 [3, 3, 320, 320], replicated, may hold values from -0.109375 to 0.109375
- conv1_bias: float32 [320], replicated, may hold values from -3 to 3
- emb_shift: float32 [4, 320], replicated, may hold values from -4 to 4
- norm2_gain: float32 [320], replicated, may hold values from 0.1 to 1.9
- norm2_shift: float32 [320], replicated, may hold values from -3 to 3
- conv2_weight: bfloat16 [3, 3, 320, 320], replicated, may hold values from -0.109375 to 0.109375
- conv2_bias: float32 [320], replicated, may hold values from -3 to 3
Outputs:
- block_out: bfloat16 [4, 64, 128, 320], P(None, 'lat', 'lon')
The draws below stay inside these ranges and needn't reach their ends.
Inputs may be any that keep to these rules, and one draw needn't show every extreme that they name: `latent`: Real-valued activations.
All inputs are finite; a program needn't handle non-finite values.
Results may differ from the reference program's by a relative error of at most 0.007.
Values may be sent and summed in bfloat16 or wider, within the bound.
No kernel may reach another device: no remote copies, remote signals or barrier semaphores. Data moves between devices by JAX's collectives and lax.ppermute only.
A program may use at most 64 MiB of HBM per device.

```python
import jax
import jax.numpy as jnp
from jax import lax

C = 320
GROUPS = 32
FRAMES = 4
LAT_ROWS = 64
LON_COLS = 128


def draw_latent(key, part):
    noise_key = jax.random.fold_in(key, 11)
    lat_key = jax.random.fold_in(key, 12)
    lon_key = jax.random.fold_in(key, 13)
    offset_key = jax.random.fold_in(key, 14)
    lat_frac = jnp.arange(LAT_ROWS, dtype=jnp.float32) / LAT_ROWS
    lon_frac = jnp.arange(LON_COLS, dtype=jnp.float32) / LON_COLS
    rough_lat = jax.random.uniform(lat_key, (LAT_ROWS,), jnp.float32, 0.8, 1.25)
    rough_lon = jax.random.uniform(lon_key, (LON_COLS,), jnp.float32, 0.8, 1.25)
    scales = 0.3 * (3.0 ** lat_frac * rough_lat)[:, None] * (3.0 ** lon_frac * rough_lon)[None, :]
    offset = jnp.clip(0.5 * jax.random.normal(offset_key, (C,), jnp.float32), -1.5, 1.5)
    noise_draw = jnp.clip(jax.random.normal(noise_key, (FRAMES, LAT_ROWS, LON_COLS, C), jnp.float32), -5.0, 5.0)
    return (scales[None, :, :, None] * (noise_draw + offset)).astype(jnp.bfloat16)


def noise(key, extent, spread, limit, held_as=jnp.bfloat16):
    entries = spread * jax.random.normal(key, extent, jnp.float32)
    return jnp.clip(entries, min=-limit, max=limit).astype(held_as)


def setup_inputs(seed: int = 0) -> dict:
    key_list = jax.random.split(jax.random.key(seed), 11)
    latent = draw_latent(jax.random.fold_in(key_list[10], 71), 0)
    norm1_gain = jnp.clip(1.0 + 0.18 * jax.random.normal(key_list[1], (C,), jnp.float32), 0.1, 1.9)
    norm1_shift = noise(key_list[2], (C,), 0.5, 3.0, jnp.float32)
    conv1_weight = noise(key_list[3], (3, 3, C, C), (9 * C) ** -0.5, 0.109375)
    conv1_bias = noise(key_list[4], (C,), 0.5, 3.0, jnp.float32)
    emb_shift = noise(key_list[5], (FRAMES, C), 1.0, 4.0, jnp.float32)
    norm2_gain = jnp.clip(1.0 + 0.18 * jax.random.normal(key_list[6], (C,), jnp.float32), 0.1, 1.9)
    norm2_shift = noise(key_list[7], (C,), 0.5, 3.0, jnp.float32)
    conv2_weight = noise(key_list[8], (3, 3, C, C), (9 * C) ** -0.5, 0.109375)
    conv2_bias = noise(key_list[9], (C,), 0.5, 3.0, jnp.float32)
    return dict(latent=latent, norm1_gain=norm1_gain, norm1_shift=norm1_shift, conv1_weight=conv1_weight, conv1_bias=conv1_bias, emb_shift=emb_shift, norm2_gain=norm2_gain, norm2_shift=norm2_shift, conv2_weight=conv2_weight, conv2_bias=conv2_bias)


def sphere_pad(field):
    half = LON_COLS // 2
    north_row = jnp.roll(field[:, :1], -half, axis=2)
    south_row = jnp.roll(field[:, -1:], -half, axis=2)
    tall_field = jnp.concatenate([north_row, field, south_row], axis=1)
    return jnp.concatenate([tall_field[:, :, -1:], tall_field, tall_field[:, :, :1]], axis=2)

def group_stats(field):
    grouped = field.reshape(FRAMES, LAT_ROWS * LON_COLS, GROUPS, C // GROUPS)
    average = lax.optimization_barrier(jnp.mean(grouped, axis=(1, 3)))
    centered = grouped - average[:, None, :, None]
    variance = lax.optimization_barrier(jnp.mean(centered * centered, axis=(1, 3)))
    return (average, lax.rsqrt(variance + 1e-05))

def activate(field, average, inverse, norm_gain, norm_shift):
    per_mean = jnp.repeat(average, C // GROUPS, axis=1)[:, None, None, :]
    per_inverse = jnp.repeat(inverse, C // GROUPS, axis=1)[:, None, None, :]
    normed = (field - per_mean) * per_inverse * norm_gain + norm_shift
    return jax.nn.silu(normed).astype(jnp.bfloat16)

def convolve(padded, weight):
    return lax.conv_general_dilated(padded.astype(jnp.float32), weight.astype(jnp.float32), (1, 1), 'VALID', dimension_numbers=('NHWC', 'HWIO', 'NHWC'), precision=lax.Precision.HIGHEST)

def reference(latent, norm1_gain, norm1_shift, conv1_weight, conv1_bias, emb_shift, norm2_gain, norm2_shift, conv2_weight, conv2_bias):
    source = latent.astype(jnp.float32)
    average, inverse = group_stats(source)
    first_act = activate(source, average, inverse, norm1_gain, norm1_shift)
    hidden = convolve(sphere_pad(first_act), conv1_weight) + conv1_bias + emb_shift[:, None, None, :]
    hidden = hidden.astype(jnp.bfloat16)
    hidden_f = hidden.astype(jnp.float32)
    average, inverse = group_stats(hidden_f)
    second_act = activate(hidden_f, average, inverse, norm2_gain, norm2_shift)
    branch = convolve(sphere_pad(second_act), conv2_weight) + conv2_bias
    return (source + branch).astype(jnp.bfloat16)
```

```python
import functools

import jax
import jax.numpy as jnp
from jax import lax
from jax.experimental import pallas as pl
from jax.experimental.pallas import tpu as pltpu
from jax.sharding import PartitionSpec as P

GROUPS = 32
EPS = 1e-05
AXES = ("lon", "lat")
F32 = jnp.float32
BF16 = jnp.bfloat16
EXACT = lax.Precision.HIGHEST
LANES = 128


def group_map(frames, channels):
    per_group = channels // GROUPS
    shape = (frames * GROUPS, channels)
    group = lax.rem(lax.broadcasted_iota(jnp.int32, shape, 0), GROUPS)
    channel = lax.broadcasted_iota(jnp.int32, shape, 1)
    low = group * per_group
    return ((channel >= low) & (channel < low + per_group)).astype(F32)


def own_lanes(frames):
    shape = (frames, frames * GROUPS)
    frame = lax.broadcasted_iota(jnp.int32, shape, 0) * GROUPS
    lane = lax.broadcasted_iota(jnp.int32, shape, 1)
    return (lane >= frame) & (lane < frame + GROUPS)


def pack(rows, groups, own):
    summed = lax.dot_general(rows, groups, (((1,), (1,)), ((), ())), precision=EXACT, preferred_element_type=F32)
    return jnp.sum(jnp.where(own, summed, 0.0), axis=0, keepdims=True)


def unpack(packed, groups, own):
    spread = jnp.where(own, jnp.broadcast_to(packed, own.shape), 0.0)
    return jnp.dot(spread, groups, precision=EXACT, preferred_element_type=F32)


def local_stats(load, frames, channels, cells, stats_ref):
    groups = group_map(frames, channels)
    own = own_lanes(frames)
    sums = jnp.concatenate(
        [jnp.sum(load(f), axis=0, keepdims=True) for f in range(frames)], axis=0
    )
    total = pack(sums, groups, own)
    mean = unpack(total * (1.0 / (cells * (channels // GROUPS))), groups, own)
    parts = []
    for f in range(frames):
        centred = load(f) - mean[f : f + 1]
        parts.append(jnp.sum(centred * centred, axis=0, keepdims=True))
    squares = pack(jnp.concatenate(parts, axis=0), groups, own)
    stats_ref[...] = jnp.broadcast_to(
        jnp.concatenate([total, squares], axis=0)[None], stats_ref.shape
    )


def merged_stats(stats_ref, local_count, frames, channels):
    groups = group_map(frames, channels)
    own = own_lanes(frames)
    stats = stats_ref[...]
    devices = stats.shape[0]
    sums, squares = stats[:, 0, :], stats[:, 1, :]
    mean = jnp.sum(sums, axis=0, keepdims=True) * (1.0 / (local_count * devices))
    apart = sums * (1.0 / local_count) - mean
    spread = jnp.sum(squares + local_count * (apart * apart), axis=0, keepdims=True)
    inverse = lax.rsqrt(spread * (1.0 / (local_count * devices)) + EPS)
    return unpack(mean, groups, own), unpack(inverse, groups, own)


def stats_kernel(x_ref, stats_ref):
    frames, height, width, channels = x_ref.shape

    def load(f):
        return x_ref[f].reshape(height * width, channels).astype(F32)

    local_stats(load, frames, channels, height * width, stats_ref)


def conv_kernel(
    last, flag_ref, x_ref, west_ref, east_ref, cw_ref, ccw_ref, stats_ref, gain_ref, shift_ref,
    weight_ref, bias_ref, *rest,
):
    if last:
        skip_ref, out_ref, act, taps, sem = rest
    else:
        out_ref, out_stats_ref, act, taps, sem = rest
    frames, height, width, channels = x_ref.shape
    main = (channels // 256) * 256
    tail = channels - main
    copies = []
    for dy in range(3):
        for dx in range(3):
            copies.append(pltpu.make_async_copy(
                weight_ref.at[dy, dx, 0:main], taps.at[dy, dx * main : (dx + 1) * main], sem.at[dy]))
            copies.append(pltpu.make_async_copy(
                weight_ref.at[dy, dx, main:channels],
                taps.at[dy, 3 * main + dx * tail : 3 * main + (dx + 1) * tail], sem.at[dy]))
    for copy in copies:
        copy.start()
    depth = 3 * channels
    if act.shape[3] > depth:
        act[:, :, :, depth:] = jnp.zeros(act.shape[:3] + (act.shape[3] - depth,), BF16)
        for dy in range(3):
            taps[dy, depth:] = jnp.zeros((taps.shape[1] - depth, channels), BF16)

    per_group = channels // GROUPS
    mean, inverse = merged_stats(stats_ref, float(height * width * per_group), frames, channels)
    scale = inverse * gain_ref[...]
    shift = shift_ref[...]
    first_is_north = flag_ref[0] == 1

    def put(f, row, dx, value):
        rows = value.shape[0]
        value = value.astype(BF16)
        act[f, row : row + rows, :, dx * main : (dx + 1) * main] = value[:, :, :main]
        at = 3 * main + dx * tail
        act[f, row : row + rows, :, at : at + tail] = value[:, :, main:]

    column = lax.broadcasted_iota(jnp.int32, (1, width, 1), 1)
    for f in range(frames):
        def activate(value):
            u = (value.astype(F32) - mean[f : f + 1]) * scale[f : f + 1] + shift
            return u / (1.0 + jnp.exp(-u))

        cw, ccw = activate(cw_ref[f]), activate(ccw_ref[f])
        north = jnp.where(first_is_north, cw, ccw)
        south = jnp.where(first_is_north, ccw, cw)
        west, east = activate(west_ref[f]), activate(east_ref[f])
        for dx in range(3):
            put(f, 0, dx, north[dx : dx + width][None])
            put(f, height + 1, dx, south[dx : dx + width][None])
        x = activate(x_ref[f].reshape(height * width, channels)).reshape(height, width, channels)
        put(f, 1, 1, x)
        left = jnp.where(column == 0, west[:, None, :], pltpu.roll(x, 1, 1))
        put(f, 1, 0, left)
        right = jnp.where(column == width - 1, east[:, None, :], pltpu.roll(x, width - 1, 1))
        put(f, 1, 2, right)

    total = None
    for dy in range(3):
        for copy in copies[6 * dy : 6 * dy + 6]:
            copy.wait()
        lhs = act[:, dy : dy + height].reshape(frames * height * width, act.shape[3])
        part = jnp.dot(lhs, taps[dy], preferred_element_type=F32)
        total = part if total is None else total + part

    cells = height * width
    for f in range(frames):
        value = total[f * cells : (f + 1) * cells] + bias_ref[f : f + 1]
        if last:
            value = value + skip_ref[f].reshape(cells, channels).astype(F32)
        out_ref[f] = value.astype(BF16).reshape(height, width, channels)
    if not last:
        def load(f):
            return out_ref[f].reshape(cells, channels).astype(F32)
        local_stats(load, frames, channels, cells, out_stats_ref)


VMEM = pl.BlockSpec(memory_space=pltpu.VMEM)
SMEM = pl.BlockSpec(memory_space=pltpu.SMEM)
ANY = pl.BlockSpec(memory_space=pl.ANY)


def call_stats(x, devices):
    frames = x.shape[0]
    return pl.pallas_call(
        stats_kernel,
        out_shape=jax.ShapeDtypeStruct((devices, 2, frames * GROUPS), F32),
        in_specs=[VMEM],
        out_specs=VMEM,
        name="first_stats",
    )(x)


def call_conv(flag, x, halo, stats, gain, shift, weight, bias, devices, skip=None):
    frames, height, width, channels = x.shape
    depth = -(-3 * channels // 256) * 256
    last = skip is not None
    out_shape = [jax.ShapeDtypeStruct(x.shape, BF16)]
    if not last:
        out_shape.append(jax.ShapeDtypeStruct((devices, 2, frames * GROUPS), F32))
    out = pl.pallas_call(
        functools.partial(conv_kernel, last),
        out_shape=out_shape,
        in_specs=[SMEM] + [VMEM] * 8 + [ANY] + [VMEM] * (2 if last else 1),
        out_specs=[VMEM] * len(out_shape),
        scratch_shapes=[
            pltpu.VMEM((frames, height + 2, width, depth), BF16),
            pltpu.VMEM((3, depth, channels), BF16),
            pltpu.SemaphoreType.DMA((3,)),
        ],
        name="second_conv" if last else "first_conv",
    )(flag, x, *halo, stats, gain[None], shift[None], weight, bias, *((skip,) if last else ()))
    return out[0] if last else out


def exchange_stats(stats):
    return lax.all_to_all(stats, AXES, 0, 0)


def halo_of(x):
    columns, rows = lax.axis_size("lon"), lax.axis_size("lat")
    half = columns // 2
    east_ring = [(k, (k + 1) % columns) for k in range(columns)]
    west_ring = [(b, a) for a, b in east_ring]
    clockwise = []
    for k in range(columns):
        for r in range(rows):
            if k < half:
                to = (k, r + 1) if r < rows - 1 else (k + half, r)
            else:
                to = (k, r - 1) if r > 0 else (k - half, r)
            clockwise.append((k * rows + r, to[0] * rows + to[1]))
    counter = [(b, a) for a, b in clockwise]
    west = lax.ppermute(x[:, :, -1], "lon", east_ring)
    east = lax.ppermute(x[:, :, 0], "lon", west_ring)

    def whole_row(i):
        return jnp.concatenate([west[:, i][:, None], x[:, i], east[:, i][:, None]], axis=1)

    downward = lax.axis_index("lon") < half
    first, final = whole_row(0), whole_row(-1)
    cw = lax.ppermute(jnp.where(downward, final, first), AXES, clockwise)
    ccw = lax.ppermute(jnp.where(downward, first, final), AXES, counter)
    return west, east, cw, ccw


def on_device(
    latent, norm1_gain, norm1_shift, conv1_weight, conv1_bias, emb_shift,
    norm2_gain, norm2_shift, conv2_weight, conv2_bias,
):
    devices = lax.axis_size("lon") * lax.axis_size("lat")
    frames, _, _, channels = latent.shape
    flag = (lax.axis_index("lon") < lax.axis_size("lon") // 2).astype(jnp.int32)[None]
    halo = halo_of(latent)
    stats = exchange_stats(call_stats(latent, devices))
    bias1 = conv1_bias[None] + emb_shift
    hidden, own = call_conv(flag, latent, halo, stats, norm1_gain, norm1_shift, conv1_weight, bias1, devices)
    halo = halo_of(hidden)
    stats = exchange_stats(own)
    bias2 = jnp.broadcast_to(conv2_bias[None], (frames, channels))
    return call_conv(flag, hidden, halo, stats, norm2_gain, norm2_shift, conv2_weight, bias2, devices, skip=latent)


def solution(mesh):
    placed = (P(None, "lat", "lon", None), P(), P(), P(), P(), P(), P(), P(), P(), P())
    return jax.shard_map(
        on_device,
        mesh=mesh,
        in_specs=placed,
        out_specs=P(None, "lat", "lon", None),
        check_vma=False,
    )
```

```python
import functools

import jax
import jax.numpy as jnp
from jax import lax
from jax.experimental import pallas as pl
from jax.experimental.pallas import tpu as pltpu
from jax.sharding import PartitionSpec as P


GROUPS = 32
EPS = 1e-05
AXES = ("lon", "lat")
F32 = jnp.float32
BF16 = jnp.bfloat16
LANES = 128
DEEP = 256
PARTS = 2
BEFORE = 3
VMEM = pl.BlockSpec(memory_space=pltpu.VMEM)
SMEM = pl.BlockSpec(memory_space=pltpu.SMEM)
HBM = pl.BlockSpec(memory_space=pltpu.MemorySpace.HBM)


def in_hbm(x):
    return pltpu.with_memory_space_constraint(x, pltpu.MemorySpace.HBM)


def group_map(frames, channels):
    per_group = channels // GROUPS
    shape = (frames * GROUPS, channels)
    group = lax.rem(lax.broadcasted_iota(jnp.int32, shape, 0), GROUPS)
    channel = lax.broadcasted_iota(jnp.int32, shape, 1)
    low = group * per_group
    return jnp.where((channel >= low) & (channel < low + per_group), 1.0, 0.0).astype(BF16)


def own_lanes(frames):
    shape = (frames, frames * GROUPS)
    frame = lax.broadcasted_iota(jnp.int32, shape, 0) * GROUPS
    lane = lax.broadcasted_iota(jnp.int32, shape, 1)
    return (lane >= frame) & (lane < frame + GROUPS)


def times_map(rows, groups, contract):
    high = rows.astype(BF16)
    rest = rows - high.astype(F32)
    middle = rest.astype(BF16)
    low = (rest - middle.astype(F32)).astype(BF16)
    return sum(
        lax.dot_general(part, groups, (((1,), (contract,)), ((), ())), preferred_element_type=F32)
        for part in (high, middle, low)
    )


def pack(rows, groups, own):
    summed = times_map(rows, groups, 1)
    return jnp.sum(jnp.where(own, summed, 0.0), axis=0, keepdims=True)


def unpack(packed, groups, own):
    return times_map(jnp.where(own, jnp.broadcast_to(packed, own.shape), 0.0), groups, 0)


def frame_sum(x_ref, f, term):
    _, height, width, channels = x_ref.shape
    total = jnp.zeros((8, channels), F32)
    for row in range(height):
        value = term(x_ref[f, row].astype(F32))
        total = total + jnp.sum(value.reshape(width // 8, 8, channels), axis=0)
    return jnp.sum(total, axis=0, keepdims=True)


def stats_kernel(x_ref, stats_ref):
    frames, height, width, channels = x_ref.shape
    sums = jnp.concatenate([frame_sum(x_ref, f, lambda v: v) for f in range(frames)], axis=0)
    groups = group_map(frames, channels)
    own = own_lanes(frames)
    total = pack(sums, groups, own)
    mean = unpack(total * (1.0 / (height * width * (channels // GROUPS))), groups, own)
    parts = []
    for f in range(frames):
        def squared(value, f=f):
            centred = value - mean[f : f + 1]
            return centred * centred

        parts.append(frame_sum(x_ref, f, squared))
    squares = pack(jnp.concatenate(parts, axis=0), groups, own)
    both = jnp.concatenate([total, squares], axis=0)
    stats_ref[...] = jnp.broadcast_to(both[None], stats_ref.shape)


def merged_stats(stats_ref, local_count, frames, channels):
    groups = group_map(frames, channels)
    own = own_lanes(frames)
    devices = stats_ref.shape[0]
    sums, squares = stats_ref[:, 0, :], stats_ref[:, 1, :]
    mean = jnp.sum(sums, axis=0, keepdims=True) * (1.0 / (local_count * devices))
    apart = sums * (1.0 / local_count) - mean
    spread = jnp.sum(squares + local_count * (apart * apart), axis=0, keepdims=True)
    inverse = lax.rsqrt(spread * (1.0 / (local_count * devices)) + EPS)
    return unpack(mean, groups, own), unpack(inverse, groups, own)


def put_edges(flag_ref, f, value, sides_ref, ends_ref):
    down, even = flag_ref[0] == 1, flag_ref[1] == 1
    first, final = value[:, 0, :], value[:, -1, :]
    sides_ref[0, f] = jnp.where(even, final, first)
    sides_ref[1, f] = jnp.where(even, first, final)
    ends_ref[0, f] = jnp.where(down, value[-1], value[0])
    ends_ref[1, f] = jnp.where(down, value[0], value[-1])


def edges_kernel(flag_ref, x_ref, copy_ref, sides_ref, ends_ref, sem):
    frames = x_ref.shape[0]
    copies = [pltpu.make_async_copy(x_ref.at[f], copy_ref.at[f], sem.at[f]) for f in range(frames)]
    for copy in copies:
        copy.start()
    for f in range(frames):
        copies[f].wait()
        put_edges(flag_ref, f, copy_ref[f], sides_ref, ends_ref)


def conv_kernel(
    last, flag_ref, x_ref, a_ref, b_ref, cw_ref, ccw_ref, stats_ref, gain_ref, shift_ref, bias_ref, extra_ref,
    weight_ref, out_ref, *rest,
):
    if last:
        staged_ref, out_sem, *rest = rest
    else:
        sides_ref, ends_ref, *rest = rest
        staged_ref = out_ref
    taps, tail_taps, side_taps, sem, *rest = rest
    grids, acts = rest[:PARTS], rest[PARTS:]
    frames, height, width, channels = x_ref.shape
    main = (channels // DEEP) * DEEP
    tail = channels - main
    tall, wide = height + 2, width + 2
    deep = tail_taps.shape[1] * tail
    lane_tiles = [(t, min(LANES, channels - t)) for t in range(0, channels, LANES)]

    copies = []
    for dy in range(3):
        copies.append((
            pltpu.make_async_copy(weight_ref.at[dy, :, 0:main], taps.at[dy], sem.at[dy, 0]),
            pltpu.make_async_copy(weight_ref.at[dy, :, main:channels], tail_taps.at[dy, 0:3], sem.at[dy, 1]),
        ))
    for pair in copies:
        for copy in pair:
            copy.start()

    def wait(dy):
        for copy in copies[dy]:
            copy.wait()

    if deep > 3 * tail:
        for dy in range(3):
            tail_taps[dy, 3:] = jnp.zeros((tail_taps.shape[1] - 3, tail, channels), BF16)
        for act in acts:
            act[:, :, :, 3 * channels :] = jnp.zeros(act.shape[:3] + (deep - 3 * tail,), BF16)

    per_group = channels // GROUPS
    mean, inverse = merged_stats(stats_ref, float(height * width * per_group), frames, channels)
    scale = inverse * (0.5 * gain_ref[...].reshape(1, channels))
    shift = 0.5 * shift_ref[...].reshape(1, channels)
    down, even = flag_ref[0] == 1, flag_ref[1] == 1
    per_part = frames // PARTS

    def prepare(f):
        grid, act, at = grids[f // per_part], acts[f // per_part], f % per_part

        def activate(value):
            part = (value.astype(F32) - mean[f : f + 1]) * scale[f : f + 1] + shift
            return part + part * jnp.tanh(part)

        def spot(row, column):
            return (at * tall + row) * wide + column

        def store(start, count, value, stride=1):
            for t, (lane, size) in enumerate(lane_tiles):
                where = pl.ds(start, count) if stride == 1 else pl.ds(start, count, stride)
                grid[t, where, 0:size] = value[:, lane : lane + size]

        cw, ccw, a, b = cw_ref[f], ccw_ref[f], a_ref[f], b_ref[f]
        store(spot(0, 0), wide, activate(jnp.where(down, cw, ccw)))
        store(spot(height + 1, 0), wide, activate(jnp.where(down, ccw, cw)))
        store(spot(1, 0), height, activate(jnp.where(even, b, a)), wide)
        store(spot(1, width + 1), height, activate(jnp.where(even, a, b)), wide)
        for row in range(height):
            store(spot(row + 1, 1), width, activate(x_ref[f, row]))
        for row in range(tall):
            for dx in range(3):
                for t, (lane, size) in enumerate(lane_tiles):
                    value = grid[t, pl.ds(spot(row, dx), width), 0:size].astype(BF16)
                    to = dx * main + lane if lane < main else 3 * main + dx * tail + lane - main
                    act[at, row, :, to : to + size] = value

    def tap(dy, low, high):
        above = taps[dy, :, :, low:high].reshape(3 * main, high - low)
        below = tail_taps[dy, :, :, low:high].reshape(deep, high - low)
        return jnp.concatenate([above, below], axis=0)

    def row_taps(part, dy):
        act = acts[part]
        lhs = act[:, dy : dy + height].reshape(per_part * height * width, act.shape[3])
        return jnp.dot(lhs, tap(dy, 0, main), preferred_element_type=F32)

    def side_of(part):
        act = acts[part]
        lhs = act[...].reshape(per_part * tall * width, act.shape[3])
        side = jnp.dot(lhs, side_taps[...], preferred_element_type=F32)
        side = side.reshape(per_part, tall, width, 3 * tail)
        return sum(side[:, dy : dy + height, :, dy * tail : (dy + 1) * tail] for dy in range(3))

    def finish(part, total, side):
        total = total.reshape(per_part, height, width, main)
        bias = bias_ref[...].reshape(1, 1, channels)
        for at in range(per_part):
            f = part * per_part + at
            for values, low, high in ((total, 0, main), (side, main, channels)):
                value = values[at] + bias[:, :, low:high]
                if last:
                    value = value + extra_ref[f, :, :, low:high].astype(F32)
                else:
                    value = value + extra_ref[f : f + 1, low:high].reshape(1, 1, high - low)
                staged_ref[f, :, :, low:high] = value.astype(BF16)
            if not last:
                put_edges(flag_ref, f, staged_ref[f], sides_ref, ends_ref)
        if last:
            span = pl.ds(part * per_part, per_part)
            pltpu.make_async_copy(staged_ref.at[span], out_ref.at[span], out_sem.at[part]).start()

    for f in range(BEFORE):
        prepare(f)
    for dy in range(3):
        wait(dy)
    for dy in range(3):
        side_taps[:, dy * tail : (dy + 1) * tail] = tap(dy, main, channels)
    for f in range(BEFORE, frames):
        prepare(f)
    for part in range(PARTS):
        finish(part, sum(row_taps(part, dy) for dy in range(3)), side_of(part))
    if last:
        for part in range(PARTS):
            span = pl.ds(part * per_part, per_part)
            pltpu.make_async_copy(staged_ref.at[span], out_ref.at[span], out_sem.at[part]).wait()


def edge_shapes(x):
    frames, height, width, channels = x.shape
    return [
        jax.ShapeDtypeStruct((2, frames, height, channels), BF16),
        jax.ShapeDtypeStruct((2, frames, width, channels), BF16),
    ]


def call_edges(flag, x):
    return pl.pallas_call(
        edges_kernel,
        out_shape=[jax.ShapeDtypeStruct(x.shape, x.dtype)] + edge_shapes(x),
        in_specs=[SMEM, HBM],
        out_specs=[VMEM] * 3,
        scratch_shapes=[pltpu.SemaphoreType.DMA((x.shape[0],))],
        name="edges",
        compiler_params=pltpu.CompilerParams(vmem_limit_bytes=8 << 20),
    )(flag, in_hbm(x))


def call_stats(x, devices):
    return pl.pallas_call(
        stats_kernel,
        out_shape=jax.ShapeDtypeStruct((devices, 2, x.shape[0] * GROUPS), F32),
        in_specs=[VMEM],
        out_specs=VMEM,
        name="own_stats",
        compiler_params=pltpu.CompilerParams(vmem_limit_bytes=8 << 20),
    )(x)


def call_conv(flag, x, halo, stats, gain, shift, weight, bias, extra, last):
    frames, height, width, channels = x.shape
    main = (channels // DEEP) * DEEP
    tail = channels - main
    slots = -(-3 * tail // DEEP) * DEEP // tail
    depth = 3 * main + slots * tail
    out_shape = [jax.ShapeDtypeStruct(x.shape, BF16)]
    cells = -(-(frames // PARTS) * (height + 2) * (width + 2) // 8) * 8
    scratch = [
        pltpu.VMEM((3, 3, main, channels), BF16),
        pltpu.VMEM((3, slots, tail, channels), BF16),
        pltpu.VMEM((depth, 3 * tail), BF16),
        pltpu.SemaphoreType.DMA((3, 2)),
    ]
    scratch += [pltpu.VMEM((-(-channels // LANES), cells, LANES), F32)] * PARTS
    scratch += [pltpu.VMEM((frames // PARTS, height + 2, width, depth), BF16)] * PARTS
    if last:
        out_specs = [HBM]
        scratch = [pltpu.VMEM(x.shape, BF16), pltpu.SemaphoreType.DMA((PARTS,))] + scratch
    else:
        out_shape += edge_shapes(x)
        out_specs = [VMEM] * 3
    out = pl.pallas_call(
        functools.partial(conv_kernel, last),
        out_shape=out_shape,
        in_specs=[SMEM] + [VMEM] * 10 + [HBM],
        out_specs=out_specs,
        scratch_shapes=scratch,
        name="second_conv" if last else "first_conv",
        compiler_params=pltpu.CompilerParams(vmem_limit_bytes=24 << 20),
    )(flag, x, *halo, stats, gain, shift, bias, extra, in_hbm(weight))
    return out[0] if last else out


def halo_of(sides, ends):
    columns, rows = lax.axis_size("lon"), lax.axis_size("lat")
    half = columns // 2
    down, even = lax.axis_index("lon") < half, lax.axis_index("lon") % 2 == 0
    paired = [(k, k ^ 1) for k in range(columns)]
    crossed = [(k, (k + 1) % columns if k % 2 else (k - 1) % columns) for k in range(columns)]
    clockwise = []
    for k in range(columns):
        for r in range(rows):
            if k < half:
                to = (k, r + 1) if r < rows - 1 else (k + half, r)
            else:
                to = (k, r - 1) if r > 0 else (k - half, r)
            clockwise.append((k * rows + r, to[0] * rows + to[1]))
    counter = [(b, a) for a, b in clockwise]
    a = lax.ppermute(sides[0], "lon", paired)
    b = lax.ppermute(sides[1], "lon", crossed)

    def whole_row(end, here):
        a_end = jnp.where(here, a[:, -1], a[:, 0])[:, None]
        b_end = jnp.where(here, b[:, -1], b[:, 0])[:, None]
        west, east = jnp.where(even, b_end, a_end), jnp.where(even, a_end, b_end)
        return jnp.concatenate([west, end, east], axis=1)

    cw = lax.ppermute(whole_row(ends[0], down), AXES, clockwise)
    ccw = lax.ppermute(whole_row(ends[1], ~down), AXES, counter)
    return a, b, cw, ccw


def gather_stats(x, devices):
    own = call_stats(x, devices)
    return lax.all_to_all(own, AXES, 0, 0)


def on_device(
    latent, norm1_gain, norm1_shift, conv1_weight, conv1_bias, emb_shift,
    norm2_gain, norm2_shift, conv2_weight, conv2_bias,
):
    devices = lax.axis_size("lon") * lax.axis_size("lat")
    column = lax.axis_index("lon")
    flag = jnp.stack([column < lax.axis_size("lon") // 2, column % 2 == 0]).astype(jnp.int32)
    latent, sides, ends = call_edges(flag, latent)
    halo = halo_of(sides, ends)
    stats = gather_stats(latent, devices)
    hidden, sides, ends = call_conv(
        flag, latent, halo, stats, norm1_gain, norm1_shift, conv1_weight, conv1_bias, emb_shift, False)
    halo = halo_of(sides, ends)
    stats = gather_stats(hidden, devices)
    return call_conv(
        flag, hidden, halo, stats, norm2_gain, norm2_shift, conv2_weight, conv2_bias, latent, True)


def solution(mesh):
    placed = (P(None, "lat", "lon", None), P(), P(), P(), P(), P(), P(), P(), P(), P())
    return jax.shard_map(
        on_device,
        mesh=mesh,
        in_specs=placed,
        out_specs=P(None, "lat", "lon", None),
        check_vma=False,
    )
```

```python
import functools

import jax
import jax.numpy as jnp
from jax import lax
from jax.experimental import pallas as pl
from jax.experimental.pallas import tpu as pltpu
from jax.sharding import PartitionSpec as P


GROUPS = 32
EPS = 1e-05
AXES = ("lon", "lat")
F32 = jnp.float32
BF16 = jnp.bfloat16
LANES = 128
DEEP = 256
PARTS = 2
VMEM = pl.BlockSpec(memory_space=pltpu.VMEM)
HBM = pl.BlockSpec(memory_space=pltpu.MemorySpace.HBM)


def in_hbm(x):
    return pltpu.with_memory_space_constraint(x, pltpu.MemorySpace.HBM)


def group_map(frames, channels):
    per_group = channels // GROUPS
    shape = (frames * GROUPS, channels)
    group = lax.rem(lax.broadcasted_iota(jnp.int32, shape, 0), GROUPS)
    channel = lax.broadcasted_iota(jnp.int32, shape, 1)
    low = group * per_group
    return jnp.where((channel >= low) & (channel < low + per_group), 1.0, 0.0).astype(BF16)


def own_lanes(frames):
    shape = (frames, frames * GROUPS)
    frame = lax.broadcasted_iota(jnp.int32, shape, 0) * GROUPS
    lane = lax.broadcasted_iota(jnp.int32, shape, 1)
    return (lane >= frame) & (lane < frame + GROUPS)


def times_map(rows, groups, contract):
    high = rows.astype(BF16)
    rest = rows - high.astype(F32)
    middle = rest.astype(BF16)
    low = (rest - middle.astype(F32)).astype(BF16)
    return sum(
        lax.dot_general(part, groups, (((1,), (contract,)), ((), ())), preferred_element_type=F32)
        for part in (high, middle, low)
    )


def pack(rows, groups, own):
    summed = times_map(rows, groups, 1)
    return jnp.sum(jnp.where(own, summed, 0.0), axis=0, keepdims=True)


def unpack(packed, groups, own):
    return times_map(jnp.where(own, jnp.broadcast_to(packed, own.shape), 0.0), groups, 0)


def frame_sum(x_ref, f, term):
    _, height, width, channels = x_ref.shape
    total = jnp.zeros((8, channels), F32)
    for row in range(height):
        value = term(x_ref[f, row].astype(F32))
        total = total + jnp.sum(value.reshape(width // 8, 8, channels), axis=0)
    return jnp.sum(total, axis=0, keepdims=True)


def frame_stats(x_ref, f):
    summed = frame_sum(x_ref, f, lambda value: value)
    mean = summed * (1.0 / (x_ref.shape[1] * x_ref.shape[2]))
    return summed, frame_sum(x_ref, f, lambda value: (value - mean) * (value - mean))


def write_stats(pairs, cells, stats_ref):
    sums = jnp.concatenate([p[0] for p in pairs], axis=0)
    squares = jnp.concatenate([p[1] for p in pairs], axis=0)
    frames, channels = sums.shape
    groups = group_map(frames, channels)
    own = own_lanes(frames)
    total = pack(sums, groups, own)
    mean = unpack(total * (1.0 / (cells * (channels // GROUPS))), groups, own)
    apart = sums * (1.0 / cells) - mean
    spread = pack(squares + cells * (apart * apart), groups, own)
    both = jnp.concatenate([total, spread], axis=0)
    stats_ref[...] = jnp.broadcast_to(both[None], stats_ref.shape)


def merged_stats(stats_ref, local_count, frames, channels):
    groups = group_map(frames, channels)
    own = own_lanes(frames)
    devices = stats_ref.shape[0]
    sums, squares = stats_ref[:, 0, :], stats_ref[:, 1, :]
    mean = jnp.sum(sums, axis=0, keepdims=True) * (1.0 / (local_count * devices))
    apart = sums * (1.0 / local_count) - mean
    spread = jnp.sum(squares + local_count * (apart * apart), axis=0, keepdims=True)
    inverse = lax.rsqrt(spread * (1.0 / (local_count * devices)) + EPS)
    return unpack(mean, groups, own), unpack(inverse, groups, own)


def place():
    column = lax.axis_index("lon")
    return column < lax.axis_size("lon") // 2, lax.rem(column, 2) == 0


def put_edges(f, value, sides_ref, ends_ref):
    down, even = place()
    first, final = value[:, 0, :], value[:, -1, :]
    sides_ref[0, f] = jnp.where(even, final, first)
    sides_ref[1, f] = jnp.where(even, first, final)
    ends_ref[0, f] = jnp.where(down, value[-1], value[0])
    ends_ref[1, f] = jnp.where(down, value[0], value[-1])


def tap_copies(weight_ref, dy, taps_ref, tails_ref, sem):
    main, tail = taps_ref.shape[1], tails_ref.shape[1]
    return (
        pltpu.make_async_copy(weight_ref.at[dy, :, 0:main], taps_ref, sem.at[0]),
        pltpu.make_async_copy(weight_ref.at[dy, :, main : main + tail], tails_ref.at[0:3], sem.at[1]),
    )


def clear_rest(tails_ref):
    if tails_ref.shape[0] > 3:
        tails_ref[3:] = jnp.zeros((tails_ref.shape[0] - 3,) + tails_ref.shape[1:], BF16)


def edges_kernel(
    x_ref, weight_ref, copy_ref, sides_ref, ends_ref, stats_ref, taps_ref, tails_ref, sem, tap_sem,
):
    frames, height, width, _ = x_ref.shape
    copies = [pltpu.make_async_copy(x_ref.at[f], copy_ref.at[f], sem.at[f]) for f in range(frames)]
    weights = tap_copies(weight_ref, 0, taps_ref, tails_ref, tap_sem)
    for copy in (*copies, *weights):
        copy.start()
    clear_rest(tails_ref)
    for copy in copies:
        copy.wait()
    pairs = []
    for f in range(frames):
        put_edges(f, copy_ref[f], sides_ref, ends_ref)
        pairs.append(frame_stats(copy_ref, f))
    write_stats(pairs, float(height * width), stats_ref)
    for copy in weights:
        copy.wait()


def conv_kernel(
    last, x_ref, a_ref, b_ref, cw_ref, ccw_ref, stats_ref, gain_ref, shift_ref, bias_ref,
    first_taps, first_tails, weight_ref, extra_ref, *rest,
):
    if last:
        out_ref, skip_ref, skip_sem, staged_ref, out_sem, *rest = rest
    else:
        next_ref, out_ref, sides_ref, ends_ref, own_stats_ref, next_taps, next_tails, next_sem, *rest = rest
        staged_ref = out_ref
    taps, tails, side_taps, sem, *rest = rest
    grids, acts, sums = rest[:PARTS], rest[PARTS : 2 * PARTS], rest[2 * PARTS :]
    frames, height, width, channels = x_ref.shape
    main = (channels // DEEP) * DEEP
    tail = channels - main
    tall, wide = height + 2, width + 2
    deep = tails.shape[1] * tail
    lane_tiles = [(t, min(LANES, channels - t)) for t in range(0, channels, LANES)]
    per_part = frames // PARTS

    copies = [
        copy for dy in (1, 2)
        for copy in tap_copies(weight_ref, dy, taps.at[dy - 1], tails.at[dy - 1], sem.at[dy - 1])
    ]
    for copy in copies:
        copy.start()
    if last:
        skip_copy = pltpu.make_async_copy(extra_ref, skip_ref, skip_sem.at[0])
        skip_copy.start()
    else:
        next_copies = tap_copies(next_ref, 0, next_taps, next_tails, next_sem)
        clear_rest(next_tails)
    for dy in (1, 2):
        clear_rest(tails.at[dy - 1])

    @pl.when(lax.axis_index("lon") >= 0)
    def _():
        if deep > 3 * tail:
            for act in acts:
                act[:, :, :, 3 * channels :] = jnp.zeros(act.shape[:3] + (deep - 3 * tail,), BF16)

        per_group = channels // GROUPS
        mean, inverse = merged_stats(stats_ref, float(height * width * per_group), frames, channels)
        scale = inverse * (0.5 * gain_ref[...].reshape(1, channels))
        shift = 0.5 * shift_ref[...].reshape(1, channels)
        down, even = place()

        def prepare(f):
            grid, act, at = grids[f // per_part], acts[f // per_part], f % per_part

            def activate(value):
                part = (value.astype(F32) - mean[f : f + 1]) * scale[f : f + 1] + shift
                return part + part * jnp.tanh(part)

            def spot(row, column):
                return (at * tall + row) * wide + column

            def store(start, count, value, stride=1):
                for t, (lane, size) in enumerate(lane_tiles):
                    where = pl.ds(start, count) if stride == 1 else pl.ds(start, count, stride)
                    grid[t, where, 0:size] = value[:, lane : lane + size]

            cw, ccw, a, b = cw_ref[f], ccw_ref[f], a_ref[f], b_ref[f]
            store(spot(0, 0), wide, activate(jnp.where(down, cw, ccw)))
            store(spot(height + 1, 0), wide, activate(jnp.where(down, ccw, cw)))
            store(spot(1, 0), height, activate(jnp.where(even, b, a)), wide)
            store(spot(1, width + 1), height, activate(jnp.where(even, a, b)), wide)
            for row in range(height):
                store(spot(row + 1, 1), width, activate(x_ref[f, row]))
            for row in range(tall):
                for dx in range(3):
                    for t, (lane, size) in enumerate(lane_tiles):
                        value = grid[t, pl.ds(spot(row, dx), width), 0:size].astype(BF16)
                        to = dx * main + lane if lane < main else 3 * main + dx * tail + lane - main
                        act[at, row, :, to : to + size] = value

        def tap(dy, low, high):
            above = taps[dy - 1, :, :, low:high] if dy else first_taps[:, :, low:high]
            below = tails[dy - 1, :, :, low:high] if dy else first_tails[:, :, low:high]
            parts = [above.reshape(3 * main, high - low), below.reshape(deep, high - low)]
            return jnp.concatenate(parts, axis=0)

        def row_taps(part, dy):
            act = acts[part]
            lhs = act[:, dy : dy + height].reshape(per_part * height * width, act.shape[3])
            return jnp.dot(lhs, tap(dy, 0, main), preferred_element_type=F32)

        def side_of(part):
            act = acts[part]
            lhs = act[...].reshape(per_part * tall * width, act.shape[3])
            side = jnp.dot(lhs, side_taps[...], preferred_element_type=F32)
            side = side.reshape(per_part, tall, width, 3 * tail)
            return sum(side[:, dy : dy + height, :, dy * tail : (dy + 1) * tail] for dy in range(3))

        def finish(part, total, side):
            total = total.reshape(per_part, height, width, main)
            bias = bias_ref[...].reshape(1, 1, channels)
            for at in range(per_part):
                f = part * per_part + at
                for values, low, high in ((total, 0, main), (side, main, channels)):
                    value = values[at] + bias[:, :, low:high]
                    if last:
                        value = value + skip_ref[f, :, :, low:high].astype(F32)
                    else:
                        value = value + extra_ref[f : f + 1, low:high].reshape(1, 1, high - low)
                    staged_ref[f, :, :, low:high] = value.astype(BF16)
                if not last:
                    put_edges(f, staged_ref[f], sides_ref, ends_ref)
                    pairs.append(frame_stats(staged_ref, f))
            if last:
                span = pl.ds(part * per_part, per_part)
                pltpu.make_async_copy(staged_ref.at[span], out_ref.at[span], out_sem.at[part]).start()

        pairs = []
        for part in range(PARTS):
            for f in range(part * per_part, (part + 1) * per_part):
                prepare(f)
            sums[part][...] = row_taps(part, 0)
        side_taps[:, 0:tail] = tap(0, main, channels)
        for dy in (1, 2):
            for copy in copies[2 * dy - 2 : 2 * dy]:
                copy.wait()
            side_taps[:, dy * tail : (dy + 1) * tail] = tap(dy, main, channels)
            if dy == 1:
                if not last:
                    for copy in next_copies:
                        copy.start()
                for part in range(PARTS):
                    sums[part][...] += row_taps(part, 1)
        if last:
            skip_copy.wait()
        for part in range(PARTS):
            finish(part, sums[part][...] + row_taps(part, 2), side_of(part))
        if last:
            for part in range(PARTS):
                span = pl.ds(part * per_part, per_part)
                pltpu.make_async_copy(staged_ref.at[span], out_ref.at[span], out_sem.at[part]).wait()
        else:
            write_stats(pairs, float(height * width), own_stats_ref)
            for copy in next_copies:
                copy.wait()


def edge_shapes(x):
    frames, height, width, channels = x.shape
    return [
        jax.ShapeDtypeStruct((2, frames, height, channels), BF16),
        jax.ShapeDtypeStruct((2, frames, width, channels), BF16),
    ]


def stats_shape(x, devices):
    return jax.ShapeDtypeStruct((devices, 2, x.shape[0] * GROUPS), F32)


def tap_shapes(channels):
    main = (channels // DEEP) * DEEP
    tail = channels - main
    slots = -(-3 * tail // DEEP) * DEEP // tail
    return (3, main, channels), (slots, tail, channels)


def call_edges(x, weight, devices):
    taps, tails = tap_shapes(x.shape[3])
    out_shape = [jax.ShapeDtypeStruct(x.shape, x.dtype), *edge_shapes(x), stats_shape(x, devices)]
    out_shape += [jax.ShapeDtypeStruct(taps, BF16), jax.ShapeDtypeStruct(tails, BF16)]
    return pl.pallas_call(
        edges_kernel,
        out_shape=out_shape,
        in_specs=[HBM, HBM],
        out_specs=[VMEM] * len(out_shape),
        scratch_shapes=[pltpu.SemaphoreType.DMA((x.shape[0],)), pltpu.SemaphoreType.DMA((2,))],
        name="edges",
        compiler_params=pltpu.CompilerParams(vmem_limit_bytes=12 << 20),
    )(in_hbm(x), in_hbm(weight))


def call_conv(x, halo, stats, gain, shift, bias, first, weight, extra, following, devices):
    frames, height, width, channels = x.shape
    main = (channels // DEEP) * DEEP
    tail = channels - main
    taps, tails = tap_shapes(channels)
    depth = 3 * main + tails[0] * tail
    last = following is None
    part = frames // PARTS
    cells = -(-part * (height + 2) * (width + 2) // 8) * 8
    scratch = [
        pltpu.VMEM((2, *taps), BF16),
        pltpu.VMEM((2, *tails), BF16),
        pltpu.VMEM((depth, 3 * tail), BF16),
        pltpu.SemaphoreType.DMA((2, 2)),
    ]
    scratch += [pltpu.VMEM((-(-channels // LANES), cells, LANES), F32)] * PARTS
    scratch += [pltpu.VMEM((part, height + 2, width, depth), BF16)] * PARTS
    scratch += [pltpu.VMEM((part * height * width, main), F32)] * PARTS
    out_shape = [jax.ShapeDtypeStruct(x.shape, BF16)]
    if last:
        out_specs = [HBM]
        operands, specs = [in_hbm(extra)], [HBM]
        scratch = [
            pltpu.VMEM(x.shape, BF16), pltpu.SemaphoreType.DMA((1,)),
            pltpu.VMEM(x.shape, BF16), pltpu.SemaphoreType.DMA((PARTS,)),
        ] + scratch
    else:
        out_shape += [*edge_shapes(x), stats_shape(x, devices)]
        out_shape += [jax.ShapeDtypeStruct(taps, BF16), jax.ShapeDtypeStruct(tails, BF16)]
        out_specs = [VMEM] * len(out_shape)
        operands, specs = [extra, in_hbm(following)], [VMEM, HBM]
        scratch = [pltpu.SemaphoreType.DMA((2,))] + scratch
    out = pl.pallas_call(
        functools.partial(conv_kernel, last),
        out_shape=out_shape,
        in_specs=[VMEM] * 11 + [HBM] + specs,
        out_specs=out_specs,
        scratch_shapes=scratch,
        name="second_conv" if last else "first_conv",
        compiler_params=pltpu.CompilerParams(vmem_limit_bytes=24 << 20),
    )(x, *halo, stats, gain, shift, bias, *first, in_hbm(weight), *operands)
    return out[0] if last else out


def halo_of(sides, ends):
    columns, rows = lax.axis_size("lon"), lax.axis_size("lat")
    half = columns // 2
    down, even = place()
    paired = [(k, k ^ 1) for k in range(columns)]
    crossed = [(k, (k + 1) % columns if k % 2 else (k - 1) % columns) for k in range(columns)]
    clockwise = []
    for k in range(columns):
        for r in range(rows):
            if k < half:
                to = (k, r + 1) if r < rows - 1 else (k + half, r)
            else:
                to = (k, r - 1) if r > 0 else (k - half, r)
            clockwise.append((k * rows + r, to[0] * rows + to[1]))
    counter = [(b, a) for a, b in clockwise]
    a = lax.ppermute(sides[0], "lon", paired)
    b = lax.ppermute(sides[1], "lon", crossed)

    def whole_row(end, here):
        a_end = jnp.where(here, a[:, -1], a[:, 0])[:, None]
        b_end = jnp.where(here, b[:, -1], b[:, 0])[:, None]
        west, east = jnp.where(even, b_end, a_end), jnp.where(even, a_end, b_end)
        return jnp.concatenate([west, end, east], axis=1)

    cw = lax.ppermute(whole_row(ends[0], down), AXES, clockwise)
    ccw = lax.ppermute(whole_row(ends[1], ~down), AXES, counter)
    return a, b, cw, ccw


def share(own):
    return lax.all_to_all(own, AXES, 0, 0)


def on_device(
    latent, norm1_gain, norm1_shift, conv1_weight, conv1_bias, emb_shift,
    norm2_gain, norm2_shift, conv2_weight, conv2_bias,
):
    devices = lax.axis_size("lon") * lax.axis_size("lat")
    held, sides, ends, own, *first = call_edges(latent, conv1_weight, devices)
    halo = halo_of(sides, ends)
    hidden, sides, ends, own, *first = call_conv(
        held, halo, share(own), norm1_gain, norm1_shift, conv1_bias, first, conv1_weight,
        emb_shift, conv2_weight, devices)
    halo = halo_of(sides, ends)
    return call_conv(
        hidden, halo, share(own), norm2_gain, norm2_shift, conv2_bias, first, conv2_weight,
        latent, None, devices)


def solution(mesh):
    placed = (P(None, "lat", "lon", None), P(), P(), P(), P(), P(), P(), P(), P(), P())
    return jax.shard_map(
        on_device,
        mesh=mesh,
        in_specs=placed,
        out_specs=P(None, "lat", "lon", None),
        check_vma=False,
    )
```

```python
import functools

import jax
import jax.numpy as jnp
from jax import lax
from jax.experimental import pallas as pl
from jax.experimental.pallas import tpu as pltpu
from jax.sharding import PartitionSpec as P


GROUPS = 32
EPS = 1e-05
AXES = ("lon", "lat")
F32 = jnp.float32
BF16 = jnp.bfloat16
LANES = 128
DEEP = 256
PARTS = 4
VMEM = pl.BlockSpec(memory_space=pltpu.VMEM)
HBM = pl.BlockSpec(memory_space=pltpu.MemorySpace.HBM)


def in_hbm(x):
    return pltpu.with_memory_space_constraint(x, pltpu.MemorySpace.HBM)


def group_map(frames, channels):
    per_group = channels // GROUPS
    shape = (GROUPS, channels)
    low = lax.broadcasted_iota(jnp.int32, shape, 0) * per_group
    channel = lax.broadcasted_iota(jnp.int32, shape, 1)
    once = jnp.where((channel >= low) & (channel < low + per_group), 1.0, 0.0).astype(BF16)
    return jnp.concatenate([once] * frames, axis=0)


def own_lanes(frames):
    shape = (frames, frames * GROUPS)
    frame = lax.broadcasted_iota(jnp.int32, shape, 0) * GROUPS
    lane = lax.broadcasted_iota(jnp.int32, shape, 1)
    return (lane >= frame) & (lane < frame + GROUPS)


def times_map(rows, groups, contract):
    high = rows.astype(BF16)
    rest = rows - high.astype(F32)
    middle = rest.astype(BF16)
    low = (rest - middle.astype(F32)).astype(BF16)
    return sum(
        lax.dot_general(part, groups, (((1,), (contract,)), ((), ())), preferred_element_type=F32)
        for part in (high, middle, low)
    )


def pack(rows, groups, own):
    summed = times_map(rows, groups, 1)
    return jnp.sum(jnp.where(own, summed, 0.0), axis=0, keepdims=True)


def unpack(packed, groups, own):
    return times_map(jnp.where(own, jnp.broadcast_to(packed, own.shape), 0.0), groups, 0)


def picker(height, width):
    shape = (2 * height + 8, height * width)
    row = lax.broadcasted_iota(jnp.int32, shape, 0)
    cell = lax.broadcasted_iota(jnp.int32, shape, 1)
    first = jnp.where(row < height, row * width, (row - height) * width + width - 1)
    return jnp.where((cell == first) | (row >= 2 * height), 1.0, 0.0).astype(BF16)


def frame_sum(x_ref, f, low, high, term):
    _, height, width, _ = x_ref.shape
    total = jnp.zeros((8, high - low), F32)
    for row in range(height):
        value = term(x_ref[f, row, :, low:high].astype(F32))
        total = total + jnp.sum(value.reshape(width // 8, 8, high - low), axis=0)
    return jnp.sum(total, axis=0, keepdims=True)


def write_stats(pairs, cells, stats_ref):
    sums = jnp.concatenate([p[0] for p in pairs], axis=0)
    squares = jnp.concatenate([p[1] for p in pairs], axis=0)
    frames, channels = sums.shape
    groups = group_map(frames, channels)
    own = own_lanes(frames)
    total = pack(sums, groups, own)
    mean = unpack(total * (1.0 / (cells * (channels // GROUPS))), groups, own)
    apart = sums * (1.0 / cells) - mean
    spread = pack(squares + cells * (apart * apart), groups, own)
    both = jnp.concatenate([total, spread], axis=0)
    stats_ref[...] = jnp.broadcast_to(both[None], stats_ref.shape)


def merged_stats(stats_ref, local_count, frames, channels):
    groups = group_map(frames, channels)
    own = own_lanes(frames)
    devices = stats_ref.shape[0]
    sums, squares = stats_ref[:, 0, :], stats_ref[:, 1, :]
    mean = jnp.sum(sums, axis=0, keepdims=True) * (1.0 / (local_count * devices))
    apart = sums * (1.0 / local_count) - mean
    spread = jnp.sum(squares + local_count * (apart * apart), axis=0, keepdims=True)
    inverse = lax.rsqrt(spread * (1.0 / (local_count * devices)) + EPS)
    return unpack(mean, groups, own), unpack(inverse, groups, own)


def place():
    column = lax.axis_index("lon")
    return column < lax.axis_size("lon") // 2, lax.rem(column, 2) == 0


def put_edges(x_ref, f, low, high, sides_ref, ends_ref, by_matmul):
    down, even = place()
    _, height, width, _ = x_ref.shape
    value = x_ref[f, :, :, low:high]
    if by_matmul:
        picked = jnp.dot(
            picker(height, width), value.reshape(height * width, high - low), preferred_element_type=F32)
        first, final = picked[0:height].astype(BF16), picked[height : 2 * height].astype(BF16)
        summed = picked[2 * height : 2 * height + 1]
    else:
        first, final = value[:, 0, :], value[:, -1, :]
        summed = frame_sum(x_ref, f, low, high, lambda v: v)
    sides_ref[0, f, :, low:high] = jnp.where(even, final, first)
    sides_ref[1, f, :, low:high] = jnp.where(even, first, final)
    ends_ref[0, f, :, low:high] = jnp.where(down, value[-1], value[0])
    ends_ref[1, f, :, low:high] = jnp.where(down, value[0], value[-1])
    mean = summed * (1.0 / (height * width))
    return summed, frame_sum(x_ref, f, low, high, lambda v: (v - mean) * (v - mean))


def tap_copies(weight_ref, dy, taps_ref, tails_ref, sem):
    main, tail = taps_ref.shape[1], tails_ref.shape[1]
    return (
        pltpu.make_async_copy(weight_ref.at[dy, :, 0:main], taps_ref, sem.at[0]),
        pltpu.make_async_copy(weight_ref.at[dy, :, main : main + tail], tails_ref.at[0:3], sem.at[1]),
    )


def clear_rest(tails_ref):
    if tails_ref.shape[0] > 3:
        tails_ref[3:] = jnp.zeros((tails_ref.shape[0] - 3,) + tails_ref.shape[1:], BF16)


def edges_kernel(
    x_ref, weight_ref, copy_ref, sides_ref, ends_ref, stats_ref, taps_ref, tails_ref, sem, tap_sem,
):
    frames, height, width, _ = x_ref.shape
    copies = [pltpu.make_async_copy(x_ref.at[f], copy_ref.at[f], sem.at[f]) for f in range(frames)]
    weights = tap_copies(weight_ref, 0, taps_ref, tails_ref, tap_sem)
    for copy in (*copies, *weights):
        copy.start()
    clear_rest(tails_ref)
    for copy in copies:
        copy.wait()
    pairs = []
    for f in range(frames):
        pairs.append(put_edges(copy_ref, f, 0, copy_ref.shape[3], sides_ref, ends_ref, True))
    write_stats(pairs, float(height * width), stats_ref)
    for copy in weights:
        copy.wait()


def conv_kernel(
    last, x_ref, a_ref, b_ref, cw_ref, ccw_ref, stats_ref, gain_ref, shift_ref, bias_ref,
    first_taps, first_tails, weight_ref, extra_ref, *rest,
):
    if last:
        out_ref, skip_ref, skip_sem, staged_ref, out_sem, *rest = rest
    else:
        next_ref, out_ref, sides_ref, ends_ref, own_stats_ref, next_taps, next_tails, next_sem, *rest = rest
        staged_ref = out_ref
    taps, tails, side_taps, sem, *rest = rest
    grids, acts, sums = rest[:PARTS], rest[PARTS : 2 * PARTS], rest[2 * PARTS :]
    frames, height, width, channels = x_ref.shape
    main = (channels // DEEP) * DEEP
    tail = channels - main
    tall, wide = height + 2, width + 2
    deep = tails.shape[1] * tail
    lane_tiles = [(t, min(LANES, channels - t)) for t in range(0, channels, LANES)]
    per_part = frames // PARTS

    copies = [
        copy for dy in (1, 2)
        for copy in tap_copies(weight_ref, dy, taps.at[dy - 1], tails.at[dy - 1], sem.at[dy - 1])
    ]
    for copy in copies:
        copy.start()
    if last:
        skip_copy = pltpu.make_async_copy(extra_ref, skip_ref, skip_sem.at[0])
        skip_copy.start()
    else:
        next_copies = tap_copies(next_ref, 0, next_taps, next_tails, next_sem)
        clear_rest(next_tails)
    for dy in (1, 2):
        clear_rest(tails.at[dy - 1])

    @pl.when(lax.axis_index("lon") >= 0)
    def _():
        if deep > 3 * tail:
            for act in acts:
                act[:, :, :, 3 * channels :] = jnp.zeros(act.shape[:3] + (deep - 3 * tail,), BF16)

        per_group = channels // GROUPS
        mean, inverse = merged_stats(stats_ref, float(height * width * per_group), frames, channels)
        scale = inverse * (0.5 * gain_ref[...].reshape(1, channels))
        shift = 0.5 * shift_ref[...].reshape(1, channels)
        down, even = place()

        def prepare(f):
            grid, act, at = grids[f // per_part], acts[f // per_part], f % per_part

            def activate(value):
                part = (value.astype(F32) - mean[f : f + 1]) * scale[f : f + 1] + shift
                return part + part * jnp.tanh(part)

            def spot(row, column):
                return (at * tall + row) * wide + column

            def store(start, count, value, stride=1):
                for t, (lane, size) in enumerate(lane_tiles):
                    where = pl.ds(start, count) if stride == 1 else pl.ds(start, count, stride)
                    grid[t, where, 0:size] = value[:, lane : lane + size]

            cw, ccw, a, b = cw_ref[f], ccw_ref[f], a_ref[f], b_ref[f]
            store(spot(0, 0), wide, activate(jnp.where(down, cw, ccw)))
            store(spot(height + 1, 0), wide, activate(jnp.where(down, ccw, cw)))
            store(spot(1, 0), height, activate(jnp.where(even, b, a)), wide)
            store(spot(1, width + 1), height, activate(jnp.where(even, a, b)), wide)
            for row in range(height):
                store(spot(row + 1, 1), width, activate(x_ref[f, row]))
            for row in range(tall):
                for dx in range(3):
                    for t, (lane, size) in enumerate(lane_tiles):
                        value = grid[t, pl.ds(spot(row, dx), width), 0:size].astype(BF16)
                        to = dx * main + lane if lane < main else 3 * main + dx * tail + lane - main
                        act[at, row, :, to : to + size] = value

        def tap(dy, low, high):
            above = taps[dy - 1, :, :, low:high] if dy else first_taps[:, :, low:high]
            below = tails[dy - 1, :, :, low:high] if dy else first_tails[:, :, low:high]
            parts = [above.reshape(3 * main, high - low), below.reshape(deep, high - low)]
            return jnp.concatenate(parts, axis=0)

        def row_taps(part, dy):
            act = acts[part]
            lhs = act[:, dy : dy + height].reshape(per_part * height * width, act.shape[3])
            return jnp.dot(lhs, tap(dy, 0, main), preferred_element_type=F32)

        def side_of(part):
            act = acts[part]
            lhs = act[...].reshape(per_part * tall * width, act.shape[3])
            side = jnp.dot(lhs, side_taps[...], preferred_element_type=F32)
            side = side.reshape(per_part, tall, width, 3 * tail)
            return sum(side[:, dy : dy + height, :, dy * tail : (dy + 1) * tail] for dy in range(3))

        def finish(part, values, low, high):
            bias = bias_ref[:].reshape(1, 1, channels)[:, :, low:high]
            for at in range(per_part):
                f = part * per_part + at
                value = values[at] + bias
                if last:
                    value = value + skip_ref[f, :, :, low:high].astype(F32)
                else:
                    value = value + extra_ref[f : f + 1, low:high].reshape(1, 1, high - low)
                staged_ref[f, :, :, low:high] = value.astype(BF16)
                if not last:
                    pairs[f].append(put_edges(staged_ref, f, low, high, sides_ref, ends_ref, False))

        pairs = [[] for _ in range(frames)]
        for part in range(PARTS):
            for f in range(part * per_part, (part + 1) * per_part):
                prepare(f)
            sums[part][...] = row_taps(part, 0)
        side_taps[:, 0:tail] = tap(0, main, channels)
        for copy in copies:
            copy.wait()
        if last:
            skip_copy.wait()
        else:
            for copy in next_copies:
                copy.start()
        for dy in (1, 2):
            side_taps[:, dy * tail : (dy + 1) * tail] = tap(dy, main, channels)
        outs = []
        for part in range(PARTS):
            total = sums[part][...] + row_taps(part, 1) + row_taps(part, 2)
            finish(part, total.reshape(per_part, height, width, main), 0, main)
            finish(part, side_of(part), main, channels)
            if last:
                span = pl.ds(part * per_part, per_part)
                outs.append(pltpu.make_async_copy(staged_ref.at[span], out_ref.at[span], out_sem.at[part]))
                outs[part].start()
        if last:
            for copy in outs:
                copy.wait()
        else:
            joined = [[jnp.concatenate(part, axis=1) for part in zip(*pair)] for pair in pairs]
            write_stats(joined, float(height * width), own_stats_ref)
            for copy in next_copies:
                copy.wait()


def edge_shapes(x):
    frames, height, width, channels = x.shape
    return [
        jax.ShapeDtypeStruct((2, frames, height, channels), BF16),
        jax.ShapeDtypeStruct((2, frames, width, channels), BF16),
    ]


def stats_shape(x, devices):
    return jax.ShapeDtypeStruct((devices, 2, x.shape[0] * GROUPS), F32)


def tap_shapes(channels):
    main = (channels // DEEP) * DEEP
    tail = channels - main
    slots = -(-3 * tail // DEEP) * DEEP // tail
    return (3, main, channels), (slots, tail, channels)


def call_edges(x, weight, devices):
    taps, tails = tap_shapes(x.shape[3])
    out_shape = [jax.ShapeDtypeStruct(x.shape, x.dtype), *edge_shapes(x), stats_shape(x, devices)]
    out_shape += [jax.ShapeDtypeStruct(taps, BF16), jax.ShapeDtypeStruct(tails, BF16)]
    return pl.pallas_call(
        edges_kernel,
        out_shape=out_shape,
        in_specs=[HBM, HBM],
        out_specs=[VMEM] * len(out_shape),
        scratch_shapes=[pltpu.SemaphoreType.DMA((x.shape[0],)), pltpu.SemaphoreType.DMA((2,))],
        name="edges",
        compiler_params=pltpu.CompilerParams(vmem_limit_bytes=12 << 20),
    )(in_hbm(x), in_hbm(weight))


def call_conv(x, halo, stats, gain, shift, bias, first, weight, extra, following, devices):
    frames, height, width, channels = x.shape
    main = (channels // DEEP) * DEEP
    tail = channels - main
    taps, tails = tap_shapes(channels)
    depth = 3 * main + tails[0] * tail
    last = following is None
    part = frames // PARTS
    cells = -(-part * (height + 2) * (width + 2) // 8) * 8 + 16
    scratch = [
        pltpu.VMEM((2, *taps), BF16),
        pltpu.VMEM((2, *tails), BF16),
        pltpu.VMEM((depth, 3 * tail), BF16),
        pltpu.SemaphoreType.DMA((2, 2)),
    ]
    scratch += [pltpu.VMEM((-(-channels // LANES), cells, LANES), F32)] * PARTS
    scratch += [pltpu.VMEM((part, height + 2, width, depth), BF16)] * PARTS
    scratch += [pltpu.VMEM((part * height * width, main), F32)] * PARTS
    out_shape = [jax.ShapeDtypeStruct(x.shape, BF16)]
    if last:
        out_specs = [HBM]
        operands, specs = [in_hbm(extra)], [HBM]
        scratch = [
            pltpu.VMEM(x.shape, BF16), pltpu.SemaphoreType.DMA((1,)),
            pltpu.VMEM(x.shape, BF16), pltpu.SemaphoreType.DMA((PARTS,)),
        ] + scratch
    else:
        out_shape += [*edge_shapes(x), stats_shape(x, devices)]
        out_shape += [jax.ShapeDtypeStruct(taps, BF16), jax.ShapeDtypeStruct(tails, BF16)]
        out_specs = [VMEM] * len(out_shape)
        operands, specs = [extra, in_hbm(following)], [VMEM, HBM]
        scratch = [pltpu.SemaphoreType.DMA((2,))] + scratch
    out = pl.pallas_call(
        functools.partial(conv_kernel, last),
        out_shape=out_shape,
        in_specs=[VMEM] * 11 + [HBM] + specs,
        out_specs=out_specs,
        scratch_shapes=scratch,
        name="second_conv" if last else "first_conv",
        compiler_params=pltpu.CompilerParams(vmem_limit_bytes=24 << 20),
    )(x, *halo, stats, gain, shift, bias, *first, in_hbm(weight), *operands)
    return out[0] if last else out


def halo_of(sides, ends):
    columns, rows = lax.axis_size("lon"), lax.axis_size("lat")
    half = columns // 2
    down, even = place()
    paired = [(k, k ^ 1) for k in range(columns)]
    crossed = [(k, (k + 1) % columns if k % 2 else (k - 1) % columns) for k in range(columns)]
    clockwise = []
    for k in range(columns):
        for r in range(rows):
            if k < half:
                to = (k, r + 1) if r < rows - 1 else (k + half, r)
            else:
                to = (k, r - 1) if r > 0 else (k - half, r)
            clockwise.append((k * rows + r, to[0] * rows + to[1]))
    counter = [(b, a) for a, b in clockwise]
    a = lax.ppermute(sides[0], "lon", paired)
    b = lax.ppermute(sides[1], "lon", crossed)

    def whole_row(end, here):
        a_end = jnp.where(here, a[:, -1], a[:, 0])[:, None]
        b_end = jnp.where(here, b[:, -1], b[:, 0])[:, None]
        west, east = jnp.where(even, b_end, a_end), jnp.where(even, a_end, b_end)
        return jnp.concatenate([west, end, east], axis=1)

    cw = lax.ppermute(whole_row(ends[0], down), AXES, clockwise)
    ccw = lax.ppermute(whole_row(ends[1], ~down), AXES, counter)
    return a, b, cw, ccw


def share(own):
    return lax.all_to_all(own, AXES, 0, 0)


def on_device(
    latent, norm1_gain, norm1_shift, conv1_weight, conv1_bias, emb_shift,
    norm2_gain, norm2_shift, conv2_weight, conv2_bias,
):
    devices = lax.axis_size("lon") * lax.axis_size("lat")
    held, sides, ends, own, *first = call_edges(latent, conv1_weight, devices)
    halo = halo_of(sides, ends)
    hidden, sides, ends, own, *first = call_conv(
        held, halo, share(own), norm1_gain, norm1_shift, conv1_bias, first, conv1_weight,
        emb_shift, conv2_weight, devices)
    halo = halo_of(sides, ends)
    return call_conv(
        hidden, halo, share(own), norm2_gain, norm2_shift, conv2_bias, first, conv2_weight,
        latent, None, devices)


def solution(mesh):
    placed = (P(None, "lat", "lon", None), P(), P(), P(), P(), P(), P(), P(), P(), P())
    return jax.shard_map(
        on_device,
        mesh=mesh,
        in_specs=placed,
        out_specs=P(None, "lat", "lon", None),
        check_vma=False,
    )
```
